128 devices in a mesh: lat: 8 (over x, core), lon: 16 (over y, z).
Axes of the slice: x: 4, y: 4, z: 4, core: 2. Of those that a mesh axis runs over, the one named last changes fastest.
Arguments:
- vorticity: float32 [16, 2, 256, 8192], P(None, None, 'lat', 'lon'), may hold values from -6 to 6
- legendre: bfloat16 [2048, 2048, 256], P(('lat', 'lon')), may hold values from -0.25 to 0.25
- wave_order: int32 [2048], replicated, may hold values from 0 to 2047, each once
Outputs:
- spectral: float32 [2048, 2, 16, 2048], P(('lat', 'lon'))
The draws below stay inside these ranges and needn't reach their ends.
Inputs may be any that keep to these rules, and one draw needn't show every extreme that they name: wave_order is a permutation: every wavenumber below 2048 is held by exactly one slot.
All inputs are finite; a program needn't handle non-finite values.
Results may differ from the reference program's by a relative error of at most 0.0029.
Values may be sent and summed in bfloat16 or wider, within the bound.
A program may use at most 128 MiB of HBM per device.

```python
import math
import jax
import jax.numpy as jnp
from jax import lax

NLON = 8192
MW = 2048
LEV = 16
LATH = 256
NDEG = 2048


def levels(key, shape, cuts, least, largest):
    factor_of, own = 1.0, jax.random.fold_in(key, 6)
    for dim, blocks in cuts:
        heights = jnp.exp(jax.random.uniform(jax.random.fold_in(own, dim), (blocks,), jnp.float32, least / len(cuts), largest / len(cuts)))
        factor_of = factor_of * jnp.repeat(heights, shape[dim] // blocks).reshape([-1 if axis == dim else 1 for axis in range(len(shape))])
    return factor_of


def bell_draw(key, dims, spread, reach, cuts=(), kind=jnp.bfloat16):
    factor_of = levels(key, dims, cuts, -0.22, 0.18) if cuts else 1.0
    drawn = jax.random.normal(key, dims, jnp.float32) * spread * factor_of
    return jnp.minimum(jnp.maximum(drawn, -reach), reach).astype(kind)


def setup_inputs(seed: int = 0) -> dict:
    arg_keys = jax.random.split(jax.random.key(seed), 4)
    vorticity = bell_draw(arg_keys[0], (LEV, 2, LATH, NLON), 1.0, 6.0, ((2, 8), (3, 16)), jnp.float32)
    legendre = bell_draw(arg_keys[1], (MW, NDEG, LATH), (2 * LATH) ** -0.5, 0.25, ((0, 128),))
    wave_order = jax.random.permutation(arg_keys[2], MW).astype(jnp.int32)
    return dict(vorticity=vorticity, legendre=legendre, wave_order=wave_order)


def reference(vorticity, legendre, wave_order):
    coefficient = jnp.fft.rfft(vorticity, axis=-1)[..., :MW] / math.sqrt(NLON)
    fourier = jnp.stack([jnp.real(coefficient), jnp.imag(coefficient)], axis=3).astype(jnp.bfloat16)
    chosen = jnp.take(fourier, wave_order, axis=4)
    per_slot = jnp.transpose(chosen, (4, 2, 1, 3, 0)).reshape(MW, LATH, 4 * LEV)
    degree = jnp.arange(NDEG, dtype=jnp.int32)
    parity = (1 - 2 * (degree % 2)).astype(jnp.float32)

    def one_slot(packed):
        table, column_data, wave = packed
        product = jnp.dot(column_data.T, table.T, preferred_element_type=jnp.float32)
        product = product.reshape(2, 2, LEV, NDEG)
        combined = product[0] + parity * product[1]
        return jnp.where(degree < MW - wave, combined, jnp.zeros_like(combined))
    return lax.map(one_slot, (legendre, per_slot, wave_order))
```

```python
import functools
import math

import jax
import jax.numpy as jnp
import numpy as np
from jax import lax
from jax.experimental import pallas as pl
from jax.experimental.pallas import tpu as pltpu
from jax.sharding import PartitionSpec as P

NLON = 8192
MW = 2048
BLOCKS = 16
SPAN = NLON // BLOCKS
HALF = MW // BLOCKS
CIRCLES = 64
ROWS = 16
MESH = pl.DeviceIdType.MESH


@functools.cache
def tables():
    n = np.arange(SPAN)
    wave = np.arange(HALF)
    phase = 2.0 * np.pi / (2 * SPAN) * (n[None, :] * (2 * wave[:, None] + 1) % (2 * SPAN))
    basis = np.concatenate([np.cos(phase), np.sin(phase)]) / math.sqrt(NLON)
    high = basis.astype(jnp.bfloat16)
    low = (basis - high.astype(np.float64)).astype(jnp.bfloat16)
    first = np.arange(BLOCKS // 2 + 1) - BLOCKS // 2
    angle = 2.0 * np.pi / NLON * (n[None, :] * first[:, None])
    twiddle = np.zeros((24, SPAN), np.float32)
    twiddle[0:9] = np.cos(angle)
    twiddle[9:18] = -np.sin(angle)
    return np.concatenate([high, low]), twiddle


def real_dft(xs):
    n = len(xs)
    if n == 2:
        return [(xs[0] + xs[1], None), (xs[0] - xs[1], None)]
    evens, odds = real_dft(xs[0::2]), real_dft(xs[1::2])
    out = [None] * (n // 2 + 1)
    for k in range(n // 4 + 1):
        (er, ei), (orr, oi) = evens[k], odds[k]
        if k == 0:
            out[0], out[n // 2] = (er + orr, None), (er - orr, None)
        elif k == n // 4:
            out[k] = (er, -orr)
        else:
            c, s = math.cos(2 * math.pi * k / n), math.sin(2 * math.pi * k / n)
            tr, ti = (c * orr, -s * orr) if oi is None else (c * orr + s * oi, c * oi - s * orr)
            out[k] = (er + tr, ti if ei is None else ei + ti)
            out[n // 2 - k] = (er - tr, ti if ei is None else ti - ei)
    return out


def split(x):
    high = x.astype(jnp.bfloat16)
    return high, (x - high.astype(jnp.float32)).astype(jnp.bfloat16)


NT = (((1,), (1,)), ((), ()))
CHUNKS = 4
CROWS = CIRCLES // CHUNKS


def fourier_kernel(
    lat_n, lon_n, order, v_hbm, basis_hbm, twiddle, out_ref,
    v_in, basis, sent, got, z_high, z_low, fourier, picked, packed,
    load_sem, send_sem, recv_sem, own_sem, out_send, out_recv, out_own,
):
    lat, lon = lax.axis_index("lat"), lax.axis_index("lon")
    v_copy = pltpu.make_async_copy(v_hbm, v_in, load_sem.at[0])
    v_copy.start()
    basis_copy = pltpu.make_async_copy(basis_hbm, basis, load_sem.at[1])
    basis_copy.start()

    barrier = pltpu.get_barrier_semaphore()
    for step in range(1, lon_n):
        peer = lax.rem(lon + step, lon_n)
        pl.semaphore_signal(barrier, inc=1, device_id=(lat, peer), device_id_type=MESH)
    for step in range(1, lat_n):
        peer = lax.rem(lat + step, lat_n)
        pl.semaphore_signal(barrier, inc=1, device_id=(peer, lon), device_id_type=MESH)

    v_copy.wait()

    @pl.loop(0, lon_n)
    def _(level):
        for c in range(CHUNKS):
            h, j = divmod(c * CROWS, 32)
            sent[level, c] = v_in[level, h, j : j + CROWS, :].astype(jnp.bfloat16)

    own = pltpu.make_async_copy(sent.at[lon], got.at[lon], own_sem)
    own.start()
    pl.semaphore_wait(barrier, lon_n - 1 + lat_n - 1)

    def exchange(c, step):
        peer = lax.rem(lon + step, lon_n)
        return pltpu.make_async_remote_copy(
            src_ref=sent.at[peer, c],
            dst_ref=got.at[lon, c],
            send_sem=send_sem.at[c],
            recv_sem=recv_sem.at[c],
            device_id=(lat, peer),
            device_id_type=MESH,
        )

    for c in range(CHUNKS):

        @pl.loop(1, lon_n)
        def _(step):
            exchange(c, step).start()

    basis_copy.wait()
    own.wait()
    for c in range(CHUNKS):
        pltpu.make_async_copy(got.at[pl.ds(1, lon_n - 1), c], got.at[pl.ds(1, lon_n - 1), c], recv_sem.at[c]).wait()

        @pl.loop(0, SPAN // 128)
        def _(part):
            lanes = pl.ds(pl.multiple_of(part * 128, 128), 128)
            blocks = [got[b, c, :, lanes].astype(jnp.float32) for b in range(BLOCKS)]
            for k, (yr, yi) in enumerate(real_dft(blocks)):
                row = k * 2 * CIRCLES + c * CROWS
                if k == BLOCKS // 2:
                    zr, zi = yr, None
                else:
                    tc, ts = twiddle[k : k + 1, lanes], twiddle[k + 9 : k + 10, lanes]
                    if yi is None:
                        zr, zi = yr * tc, yr * ts
                    else:
                        zr, zi = yr * tc - yi * ts, yr * ts + yi * tc
                high, low = split(zr)
                z_high[pl.ds(row, CROWS), lanes] = high
                z_low[pl.ds(row, CROWS), lanes] = low
                row += CIRCLES
                if zi is None:
                    high = low = jnp.zeros((CROWS, 128), jnp.bfloat16)
                else:
                    high, low = split(zi)
                z_high[pl.ds(row, CROWS), lanes] = high
                z_low[pl.ds(row, CROWS), lanes] = low

    lane = lax.broadcasted_iota(jnp.int32, (1, 128), 1)
    sign = jnp.where(lane < CIRCLES, 1.0, -1.0).astype(jnp.float32)
    for k in range(BLOCKS // 2 + 1):
        rows = pl.ds(k * 128, 128)
        by_high = lax.dot_general(basis[...], z_high[rows, :], NT, preferred_element_type=jnp.float32)
        by_low = lax.dot_general(basis[: 2 * HALF, :], z_low[rows, :], NT, preferred_element_type=jnp.float32)
        both = by_high[: 2 * HALF] + by_high[2 * HALF :] + by_low
        cos_part = both[:HALF]
        sin_part = pltpu.roll(both[HALF:], CIRCLES, 1)
        fourier[pl.ds(k, HALF, stride=BLOCKS), :] = cos_part + sign * sin_part
        if 0 < k < BLOCKS // 2:
            fourier[pl.ds(BLOCKS - k, HALF, stride=BLOCKS), :] = sign * cos_part - sin_part

    me = lat * lon_n + lon
    n = lat_n * lon_n

    @pl.loop(0, n)
    def _(step):
        to = lax.rem(me + step, n)
        base = to * ROWS
        for r in range(ROWS):
            picked[pl.ds(step * ROWS + r, 1), :] = fourier[pl.ds(order[base + r], 1), :]
        packed[step] = picked[pl.ds(pl.multiple_of(step * ROWS, ROWS), ROWS), :].astype(jnp.bfloat16)

    pltpu.make_async_copy(packed.at[0], out_ref.at[me], out_own).start()

    @pl.loop(1, n)
    def _(step):
        to = lax.rem(me + step, n)
        pltpu.make_async_remote_copy(
            src_ref=packed.at[step],
            dst_ref=out_ref.at[me],
            send_sem=out_send,
            recv_sem=out_recv,
            device_id=(to // lon_n, lax.rem(to, lon_n)),
            device_id_type=MESH,
        ).start()

    for c in range(CHUNKS):
        pltpu.make_async_copy(sent.at[pl.ds(1, lon_n - 1), c], sent.at[pl.ds(1, lon_n - 1), c], send_sem.at[c]).wait()
    pltpu.make_async_copy(packed.at[0], out_ref.at[me], out_own).wait()
    rest = packed.at[pl.ds(1, n - 1)]
    pltpu.make_async_copy(rest, rest, out_send).wait()
    pltpu.make_async_copy(rest, rest, out_recv).wait()


KB = 256


def legendre_kernel(limits, moved_ref, table, out, table_in, moved, data, result, table_sem, out_sem):
    slots, degrees, lats = table_in.shape
    parts = degrees // KB

    def fetch(s, p):
        at = pl.ds(pl.multiple_of(p * KB, KB), KB)
        return pltpu.make_async_copy(table.at[s, at], table_in.at[s, at], table_sem.at[s])

    @pl.loop(0, slots)
    def _(s):
        for p in range(parts):

            @pl.when(p * KB < limits[s])
            def _():
                fetch(s, p).start()

    @pl.loop(0, 128)
    def _(source):
        moved[pl.ds(pl.multiple_of(source * ROWS, ROWS), ROWS), :] = moved_ref[source].astype(jnp.float32)

    lane = lax.broadcasted_iota(jnp.int32, (16, 128), 1) // 32

    @pl.loop(0, slots)
    def _(s):
        for half in range(2):
            xs = [moved[pl.ds((half * 4 + i) * 256 + s, 16, stride=ROWS), :] for i in range(4)]
            for g in range(4):
                rolled = [x if i == g else pltpu.roll(x, (i - g) % 4 * 32, 1) for i, x in enumerate(xs)]
                joined = jnp.where(lane < 2, jnp.where(lane < 1, rolled[0], rolled[1]), jnp.where(lane < 3, rolled[2], rolled[3]))
                data[s, pl.ds(g * 16, 16), pl.ds(half * 128, 128)] = joined.astype(jnp.bfloat16)

    degree = lax.broadcasted_iota(jnp.int32, (1, KB), 1)
    parity = (1 - 2 * (degree % 2)).astype(jnp.float32)

    @pl.loop(0, slots)
    def _(s):
        for p in range(parts):
            at = pl.ds(p * KB, KB)
            needed = p * KB < limits[s]

            @pl.when(needed)
            def _():
                fetch(s, p).wait()
                sums = lax.dot_general(data[s], table_in[s, at, :], NT, preferred_element_type=jnp.float32)
                keep = degree + p * KB < limits[s]
                for c in range(2):
                    both = sums[c * 32 : c * 32 + 16] + parity * sums[c * 32 + 16 : c * 32 + 32]
                    result[s, c, :, at] = jnp.where(keep, both, 0.0)

            @pl.when(jnp.logical_not(needed))
            def _():
                for c in range(2):
                    result[s, c, :, at] = jnp.zeros((16, KB), jnp.float32)

        pltpu.make_async_copy(result.at[s], out.at[s], out_sem).start()

    pltpu.make_async_copy(result, out, out_sem).wait()


def on_device(vorticity, legendre, wave_order):
    lat_n, lon_n = lax.axis_size("lat"), lax.axis_size("lon")
    n = lat_n * lon_n
    basis, twiddle = tables()
    bf16, f32 = jnp.bfloat16, jnp.float32
    hbm = pl.BlockSpec(memory_space=pl.ANY)
    vmem = pl.BlockSpec(memory_space=pltpu.VMEM)
    smem = pl.BlockSpec(memory_space=pltpu.SMEM)
    dma = pltpu.SemaphoreType.DMA
    moved = pl.pallas_call(
        functools.partial(fourier_kernel, lat_n, lon_n),
        out_shape=jax.ShapeDtypeStruct((n, ROWS, 128), bf16),
        in_specs=[smem, hbm, hbm, vmem],
        out_specs=hbm,
        scratch_shapes=[
            pltpu.VMEM(vorticity.shape, f32),
            pltpu.VMEM(basis.shape, bf16),
            pltpu.VMEM((lon_n, CHUNKS, CROWS, SPAN), bf16),
            pltpu.VMEM((lon_n, CHUNKS, CROWS, SPAN), bf16),
            pltpu.VMEM((9 * 128, SPAN), bf16),
            pltpu.VMEM((9 * 128, SPAN), bf16),
            pltpu.VMEM((MW, 128), f32),
            pltpu.VMEM((MW, 128), f32),
            pltpu.VMEM((n, ROWS, 128), bf16),
            dma((2,)),
            dma((CHUNKS,)),
            dma((CHUNKS,)),
            dma,
            dma,
            dma,
            dma,
        ],
        compiler_params=pltpu.CompilerParams(collective_id=0, has_side_effects=True),
        name="fourier",
    )(wave_order, vorticity, jnp.asarray(basis), jnp.asarray(twiddle))

    first_slot = lax.axis_index(("lat", "lon")) * ROWS
    limits = MW - lax.dynamic_slice_in_dim(wave_order, first_slot, ROWS)
    slots, degrees, lats = legendre.shape
    return pl.pallas_call(
        legendre_kernel,
        out_shape=jax.ShapeDtypeStruct((slots, 2, 16, degrees), f32),
        in_specs=[smem, vmem, hbm],
        out_specs=hbm,
        scratch_shapes=[
            pltpu.VMEM(legendre.shape, bf16),
            pltpu.VMEM((MW, 128), f32),
            pltpu.VMEM((slots, 64, lats), bf16),
            pltpu.VMEM((slots, 2, 16, degrees), f32),
            dma((slots,)),
            dma,
        ],
        name="legendre_sums",
    )(limits, moved, legendre)


def solution(mesh):
    placed = (P(None, None, "lat", "lon"), P(("lat", "lon"), None, None), P())
    return jax.shard_map(
        on_device,
        mesh=mesh,
        in_specs=placed,
        out_specs=P(("lat", "lon"), None, None, None),
        check_vma=False,
    )
```

```python
import functools
import math

import jax
import jax.numpy as jnp
import numpy as np
from jax import lax
from jax.experimental import pallas as pl
from jax.experimental.pallas import tpu as pltpu
from jax.sharding import PartitionSpec as P

NLON = 8192
MW = 2048
BLOCKS = 16
SPAN = NLON // BLOCKS
HALF = MW // BLOCKS
CIRCLES = 64
ROWS = 16
MESH = pl.DeviceIdType.MESH


@functools.cache
def tables():
    n = np.arange(SPAN)
    wave = np.arange(HALF)
    phase = 2.0 * np.pi / (2 * SPAN) * (n[None, :] * (2 * wave[:, None] + 1) % (2 * SPAN))
    basis = np.concatenate([np.cos(phase), np.sin(phase)]) / math.sqrt(NLON)
    high = basis.astype(jnp.bfloat16)
    low = (basis - high.astype(np.float64)).astype(jnp.bfloat16)
    first = np.arange(BLOCKS // 2 + 1) - BLOCKS // 2
    angle = 2.0 * np.pi / NLON * (n[None, :] * first[:, None])
    twiddle = np.zeros((24, SPAN), np.float32)
    twiddle[0:9] = np.cos(angle)
    twiddle[9:18] = -np.sin(angle)
    return np.concatenate([high, low]), twiddle


def real_dft(xs):
    n = len(xs)
    if n == 2:
        return [(xs[0] + xs[1], None), (xs[0] - xs[1], None)]
    evens, odds = real_dft(xs[0::2]), real_dft(xs[1::2])
    out = [None] * (n // 2 + 1)
    for k in range(n // 4 + 1):
        (er, ei), (orr, oi) = evens[k], odds[k]
        if k == 0:
            out[0], out[n // 2] = (er + orr, None), (er - orr, None)
        elif k == n // 4:
            out[k] = (er, -orr)
        else:
            c, s = math.cos(2 * math.pi * k / n), math.sin(2 * math.pi * k / n)
            tr, ti = (c * orr, -s * orr) if oi is None else (c * orr + s * oi, c * oi - s * orr)
            out[k] = (er + tr, ti if ei is None else ei + ti)
            out[n // 2 - k] = (er - tr, ti if ei is None else ti - ei)
    return out


def split(x):
    high = x.astype(jnp.bfloat16)
    return high, (x - high.astype(jnp.float32)).astype(jnp.bfloat16)


NT = (((1,), (1,)), ((), ()))
CHUNKS = 4
CROWS = CIRCLES // CHUNKS


def fourier_kernel(
    lat_n, lon_n, order, v_hbm, basis_hbm, twiddle, out_ref,
    v_in, basis, sent, got, z_high, z_low, fourier, picked, packed,
    load_sem, send_sem, recv_sem, own_sem, out_send, out_recv, out_own,
):
    lat, lon = lax.axis_index("lat"), lax.axis_index("lon")
    v_copy = pltpu.make_async_copy(v_hbm, v_in, load_sem.at[0])
    v_copy.start()
    basis_copy = pltpu.make_async_copy(basis_hbm, basis, load_sem.at[1])
    basis_copy.start()

    barrier = pltpu.get_barrier_semaphore()
    for step in range(1, lon_n):
        peer = lax.rem(lon + step, lon_n)
        pl.semaphore_signal(barrier, inc=1, device_id=(lat, peer), device_id_type=MESH)
    for step in range(1, lat_n):
        peer = lax.rem(lat + step, lat_n)
        pl.semaphore_signal(barrier, inc=1, device_id=(peer, lon), device_id_type=MESH)

    v_copy.wait()

    @pl.loop(0, lon_n)
    def _(level):
        for c in range(CHUNKS):
            h, j = divmod(c * CROWS, 32)
            sent[level, c] = v_in[level, h, j : j + CROWS, :].astype(jnp.bfloat16)

    own = pltpu.make_async_copy(sent.at[lon], got.at[lon], own_sem)
    own.start()
    pl.semaphore_wait(barrier, lon_n - 1 + lat_n - 1)

    def exchange(c, step):
        peer = lax.rem(lon + step, lon_n)
        return pltpu.make_async_remote_copy(
            src_ref=sent.at[peer, c],
            dst_ref=got.at[lon, c],
            send_sem=send_sem.at[c],
            recv_sem=recv_sem.at[c],
            device_id=(lat, peer),
            device_id_type=MESH,
        )

    for c in range(CHUNKS):

        @pl.loop(1, lon_n)
        def _(step):
            exchange(c, step).start()

    basis_copy.wait()
    own.wait()
    for c in range(CHUNKS):
        pltpu.make_async_copy(got.at[pl.ds(1, lon_n - 1), c], got.at[pl.ds(1, lon_n - 1), c], recv_sem.at[c]).wait()

        @pl.loop(0, SPAN // 128)
        def _(part):
            lanes = pl.ds(pl.multiple_of(part * 128, 128), 128)
            blocks = [got[b, c, :, lanes].astype(jnp.float32) for b in range(BLOCKS)]
            for k, (yr, yi) in enumerate(real_dft(blocks)):
                row = k * 2 * CIRCLES + c * CROWS
                if k == BLOCKS // 2:
                    zr, zi = yr, None
                else:
                    tc, ts = twiddle[k : k + 1, lanes], twiddle[k + 9 : k + 10, lanes]
                    if yi is None:
                        zr, zi = yr * tc, yr * ts
                    else:
                        zr, zi = yr * tc - yi * ts, yr * ts + yi * tc
                high, low = split(zr)
                z_high[pl.ds(row, CROWS), lanes] = high
                z_low[pl.ds(row, CROWS), lanes] = low
                row += CIRCLES
                if zi is None:
                    high = low = jnp.zeros((CROWS, 128), jnp.bfloat16)
                else:
                    high, low = split(zi)
                z_high[pl.ds(row, CROWS), lanes] = high
                z_low[pl.ds(row, CROWS), lanes] = low

    lane = lax.broadcasted_iota(jnp.int32, (1, 128), 1)
    sign = jnp.where(lane < CIRCLES, 1.0, -1.0).astype(jnp.float32)
    for k in range(BLOCKS // 2 + 1):
        rows = pl.ds(k * 128, 128)
        by_high = lax.dot_general(basis[...], z_high[rows, :], NT, preferred_element_type=jnp.float32)
        by_low = lax.dot_general(basis[: 2 * HALF, :], z_low[rows, :], NT, preferred_element_type=jnp.float32)
        both = by_high[: 2 * HALF] + by_high[2 * HALF :] + by_low
        cos_part = both[:HALF]
        sin_part = pltpu.roll(both[HALF:], CIRCLES, 1)
        fourier[pl.ds(k, HALF, stride=BLOCKS), :] = cos_part + sign * sin_part
        if 0 < k < BLOCKS // 2:
            fourier[pl.ds(BLOCKS - k, HALF, stride=BLOCKS), :] = sign * cos_part - sin_part

    me = lat * lon_n + lon
    n = lat_n * lon_n

    for turn in range(lat_n):
        to_lat = lax.rem(lat + turn, lat_n)

        @pl.loop(0, lon_n)
        def _(step):
            base = (to_lat * lon_n + lax.rem(lon + step, lon_n)) * ROWS
            here = pl.multiple_of((turn * lon_n + step) * ROWS, ROWS)
            for r in range(ROWS):
                picked[pl.ds(here + r, 1), :] = fourier[pl.ds(order[base + r], 1), :]
            packed[turn * lon_n + step] = picked[pl.ds(here, ROWS), :].astype(jnp.bfloat16)

        if turn == 0:
            pltpu.make_async_copy(packed.at[0], out_ref.at[me], out_own).start()

        @pl.loop(0 if turn else 1, lon_n)
        def _(step):
            pltpu.make_async_remote_copy(
                src_ref=packed.at[turn * lon_n + step],
                dst_ref=out_ref.at[me],
                send_sem=out_send,
                recv_sem=out_recv,
                device_id=(to_lat, lax.rem(lon + step, lon_n)),
                device_id_type=MESH,
            ).start()

    for c in range(CHUNKS):
        pltpu.make_async_copy(sent.at[pl.ds(1, lon_n - 1), c], sent.at[pl.ds(1, lon_n - 1), c], send_sem.at[c]).wait()
    pltpu.make_async_copy(packed.at[0], out_ref.at[me], out_own).wait()
    rest = packed.at[pl.ds(1, n - 1)]
    pltpu.make_async_copy(rest, rest, out_send).wait()
    pltpu.make_async_copy(rest, rest, out_recv).wait()


KB = 256


def prepare(moved, data, s):
    lane = lax.broadcasted_iota(jnp.int32, (16, 128), 1) // 32
    for half in range(2):
        xs = [moved[pl.ds((half * 4 + i) * 256 + s, 16, stride=ROWS), :] for i in range(4)]
        for g in range(4):
            rolled = [x if i == g else pltpu.roll(x, (i - g) % 4 * 32, 1) for i, x in enumerate(xs)]
            low = jnp.where(lane < 1, rolled[0], rolled[1])
            high = jnp.where(lane < 3, rolled[2], rolled[3])
            data[s, pl.ds(g * 16, 16), pl.ds(half * 128, 128)] = jnp.where(lane < 2, low, high).astype(jnp.bfloat16)


def legendre_kernel(order, moved_ref, table, out, table_in, moved, data, result, zeros, table_sem, out_sem):
    slots, degrees, lats = table_in.shape
    parts = degrees // KB
    first = (lax.axis_index("lat") * lax.axis_size("lon") + lax.axis_index("lon")) * slots

    def blocks(s):
        return (degrees - order[first + s] + KB - 1) // KB

    def fetch(s, p):
        rows = pl.ds(0, p * KB)
        return pltpu.make_async_copy(table.at[s, rows], table_in.at[s, rows], table_sem.at[s])

    zeros[...] = jnp.zeros_like(zeros)

    @pl.loop(0, slots)
    def _(s):
        count = blocks(s)
        for p in range(1, parts + 1):

            @pl.when(count == p)
            def _():
                fetch(s, p).start()

    @pl.loop(0, 128 // 8)
    def _(group):
        for i in range(8):
            source = group * 8 + i
            moved[pl.ds(pl.multiple_of(source * ROWS, ROWS), ROWS), :] = moved_ref[source].astype(jnp.float32)

    prepare(moved, data, 0)

    @pl.loop(0, slots)
    def _(s):
        count = blocks(s)
        limit = degrees - order[first + s]
        for p in range(1, parts + 1):

            @pl.when(count == p)
            def _():
                fetch(s, p).wait()
                for q in range(p):
                    at = pl.ds(q * KB, KB)
                    sums = lax.dot_general(data[s], table_in[s, at, :], NT, preferred_element_type=jnp.float32)
                    degree = lax.broadcasted_iota(jnp.int32, (1, KB), 1)
                    parity = (1 - 2 * (degree % 2)).astype(jnp.float32)
                    for c in range(2):
                        both = sums[c * 32 : c * 32 + 16] + parity * sums[c * 32 + 16 : c * 32 + 32]
                        if q == p - 1:
                            both = jnp.where(degree + q * KB < limit, both, 0.0)
                        result[s, c, :, at] = both
                prepare(moved, data, lax.rem(s + 1, slots))
                used = pl.ds(0, p * KB)
                pltpu.make_async_copy(result.at[s, :, :, used], out.at[s, :, :, used], out_sem).start()
                if p < parts:
                    rest = pl.ds(p * KB, degrees - p * KB)
                    pltpu.make_async_copy(zeros.at[:, :, rest], out.at[s, :, :, rest], out_sem).start()

    pltpu.make_async_copy(result, out, out_sem).wait()


def on_device(vorticity, legendre, wave_order):
    lat_n, lon_n = lax.axis_size("lat"), lax.axis_size("lon")
    n = lat_n * lon_n
    basis, twiddle = tables()
    bf16, f32 = jnp.bfloat16, jnp.float32
    hbm = pl.BlockSpec(memory_space=pl.ANY)
    vmem = pl.BlockSpec(memory_space=pltpu.VMEM)
    smem = pl.BlockSpec(memory_space=pltpu.SMEM)
    dma = pltpu.SemaphoreType.DMA
    moved = pl.pallas_call(
        functools.partial(fourier_kernel, lat_n, lon_n),
        out_shape=jax.ShapeDtypeStruct((n, ROWS, 128), bf16),
        in_specs=[smem, hbm, hbm, vmem],
        out_specs=hbm,
        scratch_shapes=[
            pltpu.VMEM(vorticity.shape, f32),
            pltpu.VMEM(basis.shape, bf16),
            pltpu.VMEM((lon_n, CHUNKS, CROWS, SPAN), bf16),
            pltpu.VMEM((lon_n, CHUNKS, CROWS, SPAN), bf16),
            pltpu.VMEM((9 * 128, SPAN), bf16),
            pltpu.VMEM((9 * 128, SPAN), bf16),
            pltpu.VMEM((MW, 128), f32),
            pltpu.VMEM((MW, 128), f32),
            pltpu.VMEM((n, ROWS, 128), bf16),
            dma((2,)),
            dma((CHUNKS,)),
            dma((CHUNKS,)),
            dma,
            dma,
            dma,
            dma,
        ],
        compiler_params=pltpu.CompilerParams(collective_id=0, has_side_effects=True),
        name="fourier",
    )(wave_order, vorticity, jnp.asarray(basis), jnp.asarray(twiddle))

    slots, degrees, lats = legendre.shape
    return pl.pallas_call(
        legendre_kernel,
        out_shape=jax.ShapeDtypeStruct((slots, 2, 16, degrees), f32),
        in_specs=[smem, vmem, hbm],
        out_specs=hbm,
        scratch_shapes=[
            pltpu.VMEM(legendre.shape, bf16),
            pltpu.VMEM((MW, 128), f32),
            pltpu.VMEM((slots, 64, lats), bf16),
            pltpu.VMEM((slots, 2, 16, degrees), f32),
            pltpu.VMEM((2, 16, degrees), f32),
            dma((slots,)),
            dma,
        ],
        name="legendre_sums",
    )(wave_order, moved, legendre)


def solution(mesh):
    placed = (P(None, None, "lat", "lon"), P(("lat", "lon"), None, None), P())
    return jax.shard_map(
        on_device,
        mesh=mesh,
        in_specs=placed,
        out_specs=P(("lat", "lon"), None, None, None),
        check_vma=False,
    )
```

```python
import functools
import itertools
import math

import jax
import jax.numpy as jnp
import numpy as np
from jax import lax
from jax.experimental import pallas as pl
from jax.experimental.pallas import tpu as pltpu
from jax.sharding import PartitionSpec as P

NLON = 8192
MW = 2048
BLOCKS = 16
SPAN = NLON // BLOCKS
HALF = MW // BLOCKS
CIRCLES = 64
ROWS = 16
MESH = pl.DeviceIdType.MESH


@functools.cache
def tables():
    n = np.arange(SPAN)
    wave = np.arange(HALF)
    phase = 2.0 * np.pi / (2 * SPAN) * (n[None, :] * (2 * wave[:, None] + 1) % (2 * SPAN))
    basis = np.concatenate([np.cos(phase), np.sin(phase)]) / math.sqrt(NLON)
    high = basis.astype(jnp.bfloat16)
    low = (basis - high.astype(np.float64)).astype(jnp.bfloat16)
    first = np.arange(BLOCKS // 2 + 1) - BLOCKS // 2
    angle = 2.0 * np.pi / NLON * (n[None, :] * first[:, None])
    twiddle = np.zeros((24, SPAN), np.float32)
    twiddle[0:9] = np.cos(angle)
    twiddle[9:18] = -np.sin(angle)
    return np.concatenate([high, low]), twiddle


def real_dft(xs):
    n = len(xs)
    if n == 2:
        return [(xs[0] + xs[1], None), (xs[0] - xs[1], None)]
    evens, odds = real_dft(xs[0::2]), real_dft(xs[1::2])
    out = [None] * (n // 2 + 1)
    for k in range(n // 4 + 1):
        (er, ei), (orr, oi) = evens[k], odds[k]
        if k == 0:
            out[0], out[n // 2] = (er + orr, None), (er - orr, None)
        elif k == n // 4:
            out[k] = (er, -orr)
        else:
            c, s = math.cos(2 * math.pi * k / n), math.sin(2 * math.pi * k / n)
            tr, ti = (c * orr, -s * orr) if oi is None else (c * orr + s * oi, c * oi - s * orr)
            out[k] = (er + tr, ti if ei is None else ei + ti)
            out[n // 2 - k] = (er - tr, ti if ei is None else ti - ei)
    return out


def split(x):
    high = x.astype(jnp.bfloat16)
    return high, (x - high.astype(jnp.float32)).astype(jnp.bfloat16)


NT = (((1,), (1,)), ((), ()))
CHUNKS = 4
CROWS = CIRCLES // CHUNKS
HALVES = 2
ZROWS = 10 * 64


def fourier_kernel(
    lat_n, lon_n, order, v_hbm, basis_hbm, twiddle, out_ref,
    v_in, basis, sent, got, z_high, z_low, fourier, picked, packed,
    load_sem, send_sem, recv_sem, own_sem, out_send, out_recv, out_own,
):
    lat, lon = lax.axis_index("lat"), lax.axis_index("lon")
    v_copy = pltpu.make_async_copy(v_hbm, v_in, load_sem.at[0])
    v_copy.start()
    basis_copy = pltpu.make_async_copy(basis_hbm, basis, load_sem.at[1])
    basis_copy.start()

    x, core, y, z = lat // 2, lax.rem(lat, 2), lon // 4, lax.rem(lon, 4)
    ring = (2, 1, 3, 0)
    xs, ys, zs = ([lax.rem(at + d, 4) for d in range(4)] for at in (x, y, z))
    cores = [core, 1 - core]
    hops = lambda *shift: -sum(min(d, 4 - d) for d in shift)
    plane = sorted([(dy, dz) for dy in ring for dz in ring if dy or dz], key=lambda s: hops(*s))
    peers = [ys[dy] * 4 + zs[dz] for dy, dz in plane]

    barrier = pltpu.get_barrier_semaphore()
    for peer in peers:
        pl.semaphore_signal(barrier, inc=1, device_id=(lat, peer), device_id_type=MESH)
    for dx, dc in itertools.product(ring, (1, 0)):
        if dx or dc:
            pl.semaphore_signal(barrier, inc=1, device_id=(xs[dx] * 2 + cores[dc], lon), device_id_type=MESH)

    v_copy.wait()

    @pl.loop(0, lon_n)
    def _(level):
        for c in range(CHUNKS):
            h, j = divmod(c * CROWS, 32)
            sent[level, c] = v_in[level, h, j : j + CROWS, :].astype(jnp.bfloat16)

    own = pltpu.make_async_copy(sent.at[lon], got.at[lon], own_sem)
    own.start()
    pl.semaphore_wait(barrier, lon_n - 1 + lat_n - 1)

    for c in range(CHUNKS):
        for peer in peers:
            pltpu.make_async_remote_copy(
                src_ref=sent.at[peer, c],
                dst_ref=got.at[lon, c],
                send_sem=send_sem.at[c],
                recv_sem=recv_sem.at[c],
                device_id=(lat, peer),
                device_id_type=MESH,
            ).start()

    basis_copy.wait()
    own.wait()
    me = lat * lon_n + lon
    lane = lax.broadcasted_iota(jnp.int32, (1, 128), 1)
    real = lax.rem(lane, 64) < 32
    sign = jnp.where(real, 1.0, -1.0).astype(jnp.float32)
    for half in range(HALVES):
        empty = pl.ds(half * ZROWS + 17 * 32, ZROWS - 17 * 32)
        z_high[empty, :] = jnp.zeros((ZROWS - 17 * 32, SPAN), jnp.bfloat16)
        z_low[empty, :] = jnp.zeros((ZROWS - 17 * 32, SPAN), jnp.bfloat16)

    def first_stage(c):
        pltpu.make_async_copy(got.at[pl.ds(1, lon_n - 1), c], got.at[pl.ds(1, lon_n - 1), c], recv_sem.at[c]).wait()
        half, part_of_half = divmod(c, CHUNKS // HALVES)

        @pl.loop(0, SPAN // 128)
        def _(part):
            lanes = pl.ds(pl.multiple_of(part * 128, 128), 128)
            blocks = [got[b, c, :, lanes].astype(jnp.float32) for b in range(BLOCKS)]
            for k, (yr, yi) in enumerate(real_dft(blocks)):
                row = half * ZROWS + k * 64 + part_of_half * CROWS
                if k == BLOCKS // 2:
                    zs = [yr]
                else:
                    tc, ts = twiddle[k : k + 1, lanes], twiddle[k + 9 : k + 10, lanes]
                    if yi is None:
                        zs = [yr * tc, yr * ts]
                    else:
                        zs = [yr * tc - yi * ts, yr * ts + yi * tc]
                for i, z_part in enumerate(zs):
                    high, low = split(z_part)
                    z_high[pl.ds(row + i * 32, CROWS), lanes] = high
                    z_low[pl.ds(row + i * 32, CROWS), lanes] = low

    def second_stage(half):
        for k0, count in ((0, 4), (4, 4), (8, 2)):
            rows = pl.ds(half * ZROWS + k0 * 64, count * 64)
            by_high = lax.dot_general(basis[...], z_high[rows, :], NT, preferred_element_type=jnp.float32)
            by_low = lax.dot_general(basis[: 2 * HALF, :], z_low[rows, :], NT, preferred_element_type=jnp.float32)
            both = by_high[: 2 * HALF] + by_high[2 * HALF :] + by_low
            for pair in range(count // 2):
                at = slice(pair * 128, pair * 128 + 128)
                cos_part, sin_part = both[:HALF, at], both[HALF:, at]
                swapped = jnp.where(real, pltpu.roll(sin_part, 96, 1), pltpu.roll(sin_part, 32, 1))
                plus, minus = cos_part + sign * swapped, sign * cos_part - swapped
                k = k0 + pair * 2
                for value, first, second in ((plus, k, k + 1), (minus, BLOCKS - k, BLOCKS - k - 1)):
                    turned = pltpu.roll(value, 64, 1)
                    for wave, row in ((first, jnp.where(lane < 64, value, turned)), (second, jnp.where(lane < 64, turned, value))):
                        if (wave <= BLOCKS // 2) if value is plus else (BLOCKS // 2 < wave < BLOCKS):
                            fourier[pl.ds(wave, HALF, stride=BLOCKS), :] = row

    def send_slots(half):
        for group, (dx, dy) in enumerate(itertools.product(ring, ring)):

            @pl.loop(0, 2)
            def _(t):
                for u in range(4):
                    to_z, to_core = lax.rem(z + t * 2 + u // 2, 4), cores[u % 2]
                    base = ((xs[dx] * 2 + to_core) * lon_n + ys[dy] * 4 + to_z) * ROWS
                    here = pl.multiple_of((group * 8 + t * 4 + u) * ROWS, ROWS)
                    for r in range(ROWS):
                        picked[pl.ds(here + r, 1), :] = fourier[pl.ds(order[base + r], 1), :]
                for u in range(4):
                    here = pl.multiple_of((group * 8 + t * 4 + u) * ROWS, ROWS)
                    pair = jnp.where(lane < 64, picked[pl.ds(here, 8), :], picked[pl.ds(here + 8, 8), :])
                    packed[half, group * 8 + t * 4 + u] = pair.astype(jnp.bfloat16)

            for dz, dc in itertools.product(ring, (1, 0)):
                message = packed.at[half, group * 8 + dz * 2 + dc]
                if dx or dy or dz or dc:
                    pltpu.make_async_remote_copy(
                        src_ref=message,
                        dst_ref=out_ref.at[half, me],
                        send_sem=out_send,
                        recv_sem=out_recv,
                        device_id=(xs[dx] * 2 + cores[dc], ys[dy] * 4 + zs[dz]),
                        device_id_type=MESH,
                    ).start()
                else:
                    pltpu.make_async_copy(message, out_ref.at[half, me], out_own.at[half]).start()

    for half in range(HALVES):
        for c in range(half * CHUNKS // HALVES, (half + 1) * CHUNKS // HALVES):
            first_stage(c)
        second_stage(half)
        send_slots(half)

    for c in range(CHUNKS):
        pltpu.make_async_copy(sent.at[pl.ds(1, lon_n - 1), c], sent.at[pl.ds(1, lon_n - 1), c], send_sem.at[c]).wait()
    for half in range(HALVES):
        pltpu.make_async_copy(packed.at[half, 0], out_ref.at[half, me], out_own.at[half]).wait()
    rest = packed.at[:, pl.ds(0, lat_n * lon_n - 1)]
    pltpu.make_async_copy(rest, rest, out_send).wait()
    pltpu.make_async_copy(rest, rest, out_recv).wait()


KB = 256


def prepare(moved, data, r, half):
    lane = lax.broadcasted_iota(jnp.int32, (16, 128), 1) // 32
    for k in range(2):
        xs = [moved[pl.ds(half * 1024 + (k * 4 + i) * 128 + r, 16, stride=8), :] for i in range(4)]
        for g in range(4):
            rolled = [x if i == g else pltpu.roll(x, (i - g) % 4 * 32, 1) for i, x in enumerate(xs)]
            low = jnp.where(lane < 1, rolled[0], rolled[1])
            high = jnp.where(lane < 3, rolled[2], rolled[3])
            rows = pl.ds(pl.multiple_of((g % 2 * 2 + half) * 16, 16), 16)
            data[g // 2 * 8 + r, rows, pl.ds(k * 128, 128)] = jnp.where(lane < 2, low, high).astype(jnp.bfloat16)


def legendre_kernel(order, moved_ref, table, out, table_in, moved, data, result, zeros, table_sem, out_sem):
    slots, degrees, lats = table_in.shape
    parts = degrees // KB
    first = (lax.axis_index("lat") * lax.axis_size("lon") + lax.axis_index("lon")) * slots

    def blocks(s):
        return (degrees - order[first + s] + KB - 1) // KB

    def fetch(s, p):
        rows = pl.ds(0, p * KB)
        return pltpu.make_async_copy(table.at[s, rows], table_in.at[s, rows], table_sem.at[s])

    zeros[...] = jnp.zeros_like(zeros)

    @pl.loop(0, slots)
    def _(t):
        s = lax.rem(t, 2) * 8 + t // 2
        count = blocks(s)
        for p in range(1, parts + 1):

            @pl.when(count == p)
            def _():
                fetch(s, p).start()

    for half in range(HALVES):

        @pl.loop(0, 128 // 16)
        def _(group):
            for i in range(16):
                source = group * 16 + i
                row = pl.multiple_of(half * 1024 + source * 8, 8)
                moved[pl.ds(row, 8), :] = moved_ref[half, source].astype(jnp.float32)

        prepare(moved, data, 0, half)

    @pl.loop(0, slots)
    def _(t):
        half, pair = lax.rem(t, 2), t // 2
        s = half * 8 + pair
        count = blocks(s)
        limit = degrees - order[first + s]
        for p in range(1, parts + 1):

            @pl.when(count == p)
            def _():
                fetch(s, p).wait()
                for q in range(p):
                    at = pl.ds(q * KB, KB)
                    sums = lax.dot_general(data[s], table_in[s, at, :], NT, preferred_element_type=jnp.float32)
                    degree = lax.broadcasted_iota(jnp.int32, (1, KB), 1)
                    parity = (1 - 2 * (degree % 2)).astype(jnp.float32)
                    for c in range(2):
                        both = sums[c * 32 : c * 32 + 16] + parity * sums[c * 32 + 16 : c * 32 + 32]
                        if q == p - 1:
                            both = jnp.where(degree + q * KB < limit, both, 0.0)
                        result[s, c, :, at] = both
                prepare(moved, data, lax.rem(pair + 1, 8), half)
                used = pl.ds(0, p * KB)
                pltpu.make_async_copy(result.at[s, :, :, used], out.at[s, :, :, used], out_sem).start()
                if p < parts:
                    rest = pl.ds(p * KB, degrees - p * KB)
                    pltpu.make_async_copy(zeros.at[:, :, rest], out.at[s, :, :, rest], out_sem).start()

    pltpu.make_async_copy(result, out, out_sem).wait()


def on_device(vorticity, legendre, wave_order):
    lat_n, lon_n = lax.axis_size("lat"), lax.axis_size("lon")
    n = lat_n * lon_n
    basis, twiddle = tables()
    bf16, f32 = jnp.bfloat16, jnp.float32
    hbm = pl.BlockSpec(memory_space=pl.ANY)
    vmem = pl.BlockSpec(memory_space=pltpu.VMEM)
    smem = pl.BlockSpec(memory_space=pltpu.SMEM)
    dma = pltpu.SemaphoreType.DMA
    moved = pl.pallas_call(
        functools.partial(fourier_kernel, lat_n, lon_n),
        out_shape=jax.ShapeDtypeStruct((HALVES, n, ROWS // 2, 128), bf16),
        in_specs=[smem, hbm, hbm, vmem],
        out_specs=hbm,
        scratch_shapes=[
            pltpu.VMEM(vorticity.shape, f32),
            pltpu.VMEM(basis.shape, bf16),
            pltpu.VMEM((lon_n, CHUNKS, CROWS, SPAN), bf16),
            pltpu.VMEM((lon_n, CHUNKS, CROWS, SPAN), bf16),
            pltpu.VMEM((HALVES * ZROWS, SPAN), bf16),
            pltpu.VMEM((HALVES * ZROWS, SPAN), bf16),
            pltpu.VMEM((MW, 128), f32),
            pltpu.VMEM((MW, 128), f32),
            pltpu.VMEM((HALVES, n, ROWS // 2, 128), bf16),
            dma((2,)),
            dma((CHUNKS,)),
            dma((CHUNKS,)),
            dma,
            dma,
            dma,
            dma((HALVES,)),
        ],
        compiler_params=pltpu.CompilerParams(collective_id=0, has_side_effects=True),
        name="fourier",
    )(wave_order, vorticity, jnp.asarray(basis), jnp.asarray(twiddle))

    slots, degrees, lats = legendre.shape
    return pl.pallas_call(
        legendre_kernel,
        out_shape=jax.ShapeDtypeStruct((slots, 2, 16, degrees), f32),
        in_specs=[smem, vmem, hbm],
        out_specs=hbm,
        scratch_shapes=[
            pltpu.VMEM(legendre.shape, bf16),
            pltpu.VMEM((MW, 128), f32),
            pltpu.VMEM((slots, 64, lats), bf16),
            pltpu.VMEM((slots, 2, 16, degrees), f32),
            pltpu.VMEM((2, 16, degrees), f32),
            dma((slots,)),
            dma,
        ],
        name="legendre_sums",
    )(wave_order, moved, legendre)


def solution(mesh):
    placed = (P(None, None, "lat", "lon"), P(("lat", "lon"), None, None), P())
    return jax.shard_map(
        on_device,
        mesh=mesh,
        in_specs=placed,
        out_specs=P(("lat", "lon"), None, None, None),
        check_vma=False,
    )
```

```python
import functools
import itertools
import math

import jax
import jax.numpy as jnp
import numpy as np
from jax import lax
from jax.experimental import pallas as pl
from jax.experimental.pallas import tpu as pltpu
from jax.sharding import PartitionSpec as P

NLON = 8192
MW = 2048
BLOCKS = 16
SPAN = NLON // BLOCKS
HALF = MW // BLOCKS
CIRCLES = 64
ROWS = 16
MESH = pl.DeviceIdType.MESH


@functools.cache
def tables():
    n = np.arange(SPAN)
    wave = np.arange(HALF)
    phase = 2.0 * np.pi / (2 * SPAN) * (n[None, :] * (2 * wave[:, None] + 1) % (2 * SPAN))
    basis = np.concatenate([np.cos(phase), np.sin(phase)]) / math.sqrt(NLON)
    high = basis.astype(jnp.bfloat16)
    low = (basis - high.astype(np.float64)).astype(jnp.bfloat16)
    first = np.arange(BLOCKS // 2 + 1) - BLOCKS // 2
    angle = 2.0 * np.pi / NLON * (n[None, :] * first[:, None])
    twiddle = np.zeros((24, SPAN), np.float32)
    twiddle[0:9] = np.cos(angle)
    twiddle[9:18] = -np.sin(angle)
    return np.concatenate([high, low]), twiddle


def real_dft(xs):
    n = len(xs)
    if n == 2:
        return [(xs[0] + xs[1], None), (xs[0] - xs[1], None)]
    evens, odds = real_dft(xs[0::2]), real_dft(xs[1::2])
    out = [None] * (n // 2 + 1)
    for k in range(n // 4 + 1):
        (er, ei), (orr, oi) = evens[k], odds[k]
        if k == 0:
            out[0], out[n // 2] = (er + orr, None), (er - orr, None)
        elif k == n // 4:
            out[k] = (er, -orr)
        else:
            c, s = math.cos(2 * math.pi * k / n), math.sin(2 * math.pi * k / n)
            tr, ti = (c * orr, -s * orr) if oi is None else (c * orr + s * oi, c * oi - s * orr)
            out[k] = (er + tr, ti if ei is None else ei + ti)
            out[n // 2 - k] = (er - tr, ti if ei is None else ti - ei)
    return out


def split(x):
    high = x.astype(jnp.bfloat16)
    return high, (x - high.astype(jnp.float32)).astype(jnp.bfloat16)


NT = (((1,), (1,)), ((), ()))
CHUNKS = 4
CROWS = CIRCLES // CHUNKS
HALVES = 2
GRANT = 49_737_728
ZROWS = 10 * 64


def fourier_kernel(
    lat_n, lon_n, order, v_hbm, basis_hbm, twiddle, table_hbm, out_ref, table_ref,
    v_in, basis, sent, got, z_high, z_low, fourier, picked, packed,
    load_sem, send_sem, recv_sem, own_sem, out_send, out_recv, out_own,
):
    lat, lon = lax.axis_index("lat"), lax.axis_index("lon")
    v_copy = pltpu.make_async_copy(v_hbm, v_in, load_sem.at[0])
    v_copy.start()
    basis_copy = pltpu.make_async_copy(basis_hbm, basis, load_sem.at[1])
    basis_copy.start()

    x, core, y, z = lat // 2, lax.rem(lat, 2), lon // 4, lax.rem(lon, 4)
    ring = (2, 1, 3, 0)
    xs, ys, zs = ([lax.rem(at + d, 4) for d in range(4)] for at in (x, y, z))
    cores = [core, 1 - core]
    hops = lambda *shift: -sum(min(d, 4 - d) for d in shift)
    plane = sorted([(dy, dz) for dy in ring for dz in ring if dy or dz], key=lambda s: hops(*s))
    peers = [ys[dy] * 4 + zs[dz] for dy, dz in plane]

    barrier = pltpu.get_barrier_semaphore()
    for peer in peers:
        pl.semaphore_signal(barrier, inc=1, device_id=(lat, peer), device_id_type=MESH)
    for dx, dc in itertools.product(ring, (1, 0)):
        if dx or dc:
            pl.semaphore_signal(barrier, inc=1, device_id=(xs[dx] * 2 + cores[dc], lon), device_id_type=MESH)

    v_copy.wait()
    table_copy = pltpu.make_async_copy(table_hbm, table_ref, load_sem.at[2])
    table_copy.start()

    @pl.loop(0, lon_n)
    def _(level):
        for c in range(CHUNKS):
            h, j = divmod(c * CROWS, 32)
            sent[level, c] = v_in[level, h, j : j + CROWS, :].astype(jnp.bfloat16)

    own = pltpu.make_async_copy(sent.at[lon], got.at[lon], own_sem)
    own.start()
    pl.semaphore_wait(barrier, lon_n - 1 + lat_n - 1)

    for c in range(CHUNKS):
        for peer in peers:
            pltpu.make_async_remote_copy(
                src_ref=sent.at[peer, c],
                dst_ref=got.at[lon, c],
                send_sem=send_sem.at[c],
                recv_sem=recv_sem.at[c],
                device_id=(lat, peer),
                device_id_type=MESH,
            ).start()

    basis_copy.wait()
    own.wait()
    me = lat * lon_n + lon
    lane = lax.broadcasted_iota(jnp.int32, (1, 128), 1)
    real = lax.rem(lane, 64) < 32
    sign = jnp.where(real, 1.0, -1.0).astype(jnp.float32)
    for half in range(HALVES):
        empty = pl.ds(half * ZROWS + 17 * 32, ZROWS - 17 * 32)
        z_high[empty, :] = jnp.zeros((ZROWS - 17 * 32, SPAN), jnp.bfloat16)
        z_low[empty, :] = jnp.zeros((ZROWS - 17 * 32, SPAN), jnp.bfloat16)

    def first_stage(c):
        pltpu.make_async_copy(got.at[pl.ds(1, lon_n - 1), c], got.at[pl.ds(1, lon_n - 1), c], recv_sem.at[c]).wait()
        half, part_of_half = divmod(c, CHUNKS // HALVES)

        @pl.loop(0, SPAN // 128)
        def _(part):
            lanes = pl.ds(pl.multiple_of(part * 128, 128), 128)
            blocks = [got[b, c, :, lanes].astype(jnp.float32) for b in range(BLOCKS)]
            for k, (yr, yi) in enumerate(real_dft(blocks)):
                row = half * ZROWS + k * 64 + part_of_half * CROWS
                if k == BLOCKS // 2:
                    zs = [yr]
                else:
                    tc, ts = twiddle[k : k + 1, lanes], twiddle[k + 9 : k + 10, lanes]
                    if yi is None:
                        zs = [yr * tc, yr * ts]
                    else:
                        zs = [yr * tc - yi * ts, yr * ts + yi * tc]
                for i, z_part in enumerate(zs):
                    high, low = split(z_part)
                    z_high[pl.ds(row + i * 32, CROWS), lanes] = high
                    z_low[pl.ds(row + i * 32, CROWS), lanes] = low

    def second_stage(half):
        for k0, count in ((0, 4), (4, 4), (8, 2)):
            rows = pl.ds(half * ZROWS + k0 * 64, count * 64)
            by_high = lax.dot_general(basis[...], z_high[rows, :], NT, preferred_element_type=jnp.float32)
            by_low = lax.dot_general(basis[: 2 * HALF, :], z_low[rows, :], NT, preferred_element_type=jnp.float32)
            both = by_high[: 2 * HALF] + by_high[2 * HALF :] + by_low
            for pair in range(count // 2):
                at = slice(pair * 128, pair * 128 + 128)
                cos_part, sin_part = both[:HALF, at], both[HALF:, at]
                swapped = jnp.where(real, pltpu.roll(sin_part, 96, 1), pltpu.roll(sin_part, 32, 1))
                plus, minus = cos_part + sign * swapped, sign * cos_part - swapped
                k = k0 + pair * 2
                for value, first, second in ((plus, k, k + 1), (minus, BLOCKS - k, BLOCKS - k - 1)):
                    turned = pltpu.roll(value, 64, 1)
                    for wave, row in ((first, jnp.where(lane < 64, value, turned)), (second, jnp.where(lane < 64, turned, value))):
                        if (wave <= BLOCKS // 2) if value is plus else (BLOCKS // 2 < wave < BLOCKS):
                            fourier[pl.ds(wave, HALF, stride=BLOCKS), :] = row

    def gather(half, group):
        dx, dy = groups[group]

        @pl.loop(0, 2)
        def _(t):
            for u in range(4):
                to_z, to_core = lax.rem(z + t * 2 + u // 2, 4), cores[u % 2]
                base = ((xs[dx] * 2 + to_core) * lon_n + ys[dy] * 4 + to_z) * ROWS
                here = pl.multiple_of((group * 8 + t * 4 + u) * ROWS, ROWS)
                for r in range(ROWS):
                    picked[pl.ds(here + r, 1), :] = fourier[pl.ds(order[base + r], 1), :]
            for u in range(4):
                here = pl.multiple_of((group * 8 + t * 4 + u) * ROWS, ROWS)
                pair = jnp.where(lane < 64, picked[pl.ds(here, 8), :], picked[pl.ds(here + 8, 8), :])
                packed[half, group * 8 + t * 4 + u] = pair.astype(jnp.bfloat16)

    def send(half, group):
        dx, dy = groups[group]
        for dz, dc in itertools.product(ring, (1, 0)):
            message = packed.at[half, group * 8 + dz * 2 + dc]
            if dx or dy or dz or dc:
                pltpu.make_async_remote_copy(
                    src_ref=message,
                    dst_ref=out_ref.at[half, me],
                    send_sem=out_send,
                    recv_sem=out_recv,
                    device_id=(xs[dx] * 2 + cores[dc], ys[dy] * 4 + zs[dz]),
                    device_id_type=MESH,
                ).start()
            else:
                pltpu.make_async_copy(message, out_ref.at[half, me], out_own.at[half]).start()

    groups = list(itertools.product(ring, ring))
    first_stage(0)
    first_stage(1)
    second_stage(0)
    for g in range(16):
        gather(0, g)
    first_stage(2)
    for g in range(16):
        send(0, g)
    first_stage(3)
    second_stage(1)
    for g in range(16):
        gather(1, g)
        send(1, g)

    for c in range(CHUNKS):
        pltpu.make_async_copy(sent.at[pl.ds(1, lon_n - 1), c], sent.at[pl.ds(1, lon_n - 1), c], send_sem.at[c]).wait()
    for half in range(HALVES):
        pltpu.make_async_copy(packed.at[half, 0], out_ref.at[half, me], out_own.at[half]).wait()
    rest = packed.at[:, pl.ds(0, lat_n * lon_n - 1)]
    pltpu.make_async_copy(rest, rest, out_send).wait()
    pltpu.make_async_copy(rest, rest, out_recv).wait()
    table_copy.wait()


KB = 256


def prepare(moved, data, r, half):
    lane = lax.broadcasted_iota(jnp.int32, (16, 128), 1) // 32
    for k in range(2):
        xs = [moved[pl.ds(half * 1024 + (k * 4 + i) * 128 + r, 16, stride=8), :] for i in range(4)]
        for g in range(4):
            rolled = [x if i == g else pltpu.roll(x, (i - g) % 4 * 32, 1) for i, x in enumerate(xs)]
            low = jnp.where(lane < 1, rolled[0], rolled[1])
            high = jnp.where(lane < 3, rolled[2], rolled[3])
            rows = pl.ds(pl.multiple_of((g % 2 * 2 + half) * 16, 16), 16)
            data[g // 2 * 8 + r, rows, pl.ds(k * 128, 128)] = jnp.where(lane < 2, low, high).astype(jnp.bfloat16)


def legendre_kernel(order_hbm, moved_ref, table_in, out, order, moved, data, result, zeros, order_sem, out_sem):
    slots, degrees, lats = table_in.shape
    parts = degrees // KB
    first = (lax.axis_index("lat") * lax.axis_size("lon") + lax.axis_index("lon")) * slots

    def blocks(s):
        return (degrees - order[first + s] + KB - 1) // KB

    order_copy = pltpu.make_async_copy(order_hbm, order, order_sem)
    order_copy.start()
    zeros[...] = jnp.zeros_like(zeros)

    for half in range(HALVES):

        @pl.loop(0, 128 // 16)
        def _(group):
            for i in range(16):
                source = group * 16 + i
                row = pl.multiple_of(half * 1024 + source * 8, 8)
                moved[pl.ds(row, 8), :] = moved_ref[half, source].astype(jnp.float32)

        prepare(moved, data, 0, half)

    order_copy.wait()

    @pl.loop(0, slots)
    def _(t):
        half, pair = lax.rem(t, 2), t // 2
        s = half * 8 + pair
        count = blocks(s)
        limit = degrees - order[first + s]
        for p in range(1, parts + 1):

            @pl.when(count == p)
            def _():
                for q in range(p):
                    at = pl.ds(q * KB, KB)
                    sums = lax.dot_general(data[s], table_in[s, at, :], NT, preferred_element_type=jnp.float32)
                    degree = lax.broadcasted_iota(jnp.int32, (1, KB), 1)
                    parity = (1 - 2 * (degree % 2)).astype(jnp.float32)
                    for c in range(2):
                        both = sums[c * 32 : c * 32 + 16] + parity * sums[c * 32 + 16 : c * 32 + 32]
                        if q == p - 1:
                            both = jnp.where(degree + q * KB < limit, both, 0.0)
                        result[s, c, :, at] = both
                prepare(moved, data, lax.rem(pair + 1, 8), half)
                used = pl.ds(0, p * KB)
                pltpu.make_async_copy(result.at[s, :, :, used], out.at[s, :, :, used], out_sem).start()
                if p < parts:
                    rest = pl.ds(p * KB, degrees - p * KB)
                    pltpu.make_async_copy(zeros.at[:, :, rest], out.at[s, :, :, rest], out_sem).start()

    pltpu.make_async_copy(result, out, out_sem).wait()


def on_device(vorticity, legendre, wave_order):
    lat_n, lon_n = lax.axis_size("lat"), lax.axis_size("lon")
    n = lat_n * lon_n
    basis, twiddle = tables()
    bf16, f32 = jnp.bfloat16, jnp.float32
    hbm = pl.BlockSpec(memory_space=pl.ANY)
    vmem = pl.BlockSpec(memory_space=pltpu.VMEM)
    smem = pl.BlockSpec(memory_space=pltpu.SMEM)
    dma = pltpu.SemaphoreType.DMA
    moved, table = pl.pallas_call(
        functools.partial(fourier_kernel, lat_n, lon_n),
        out_shape=(pltpu.VMEM((HALVES, n, ROWS // 2, 128), bf16), pltpu.VMEM(legendre.shape, bf16)),
        in_specs=[smem, hbm, hbm, vmem, hbm],
        out_specs=(vmem, vmem),
        scratch_shapes=[
            pltpu.VMEM(vorticity.shape, f32),
            pltpu.VMEM(basis.shape, bf16),
            pltpu.VMEM((lon_n, CHUNKS, CROWS, SPAN), bf16),
            pltpu.VMEM((lon_n, CHUNKS, CROWS, SPAN), bf16),
            pltpu.VMEM((HALVES * ZROWS, SPAN), bf16),
            pltpu.VMEM((HALVES * ZROWS, SPAN), bf16),
            pltpu.VMEM((MW, 128), f32),
            pltpu.VMEM((MW, 128), f32),
            pltpu.VMEM((HALVES, n, ROWS // 2, 128), bf16),
            dma((3,)),
            dma((CHUNKS,)),
            dma((CHUNKS,)),
            dma,
            dma,
            dma,
            dma((HALVES,)),
        ],
        compiler_params=pltpu.CompilerParams(collective_id=0, has_side_effects=True, vmem_limit_bytes=GRANT),
        name="fourier",
    )(wave_order, vorticity, jnp.asarray(basis), jnp.asarray(twiddle), legendre)

    slots, degrees, lats = legendre.shape
    moved = pltpu.with_memory_space_constraint(moved, pltpu.VMEM)
    table = pltpu.with_memory_space_constraint(table, pltpu.VMEM)
    return pl.pallas_call(
        legendre_kernel,
        out_shape=jax.ShapeDtypeStruct((slots, 2, 16, degrees), f32),
        in_specs=[hbm, vmem, vmem],
        out_specs=hbm,
        scratch_shapes=[
            pltpu.SMEM(wave_order.shape, jnp.int32),
            pltpu.VMEM((MW, 128), f32),
            pltpu.VMEM((slots, 64, lats), bf16),
            pltpu.VMEM((slots, 2, 16, degrees), f32),
            pltpu.VMEM((2, 16, degrees), f32),
            dma,
            dma,
        ],
        compiler_params=pltpu.CompilerParams(vmem_limit_bytes=GRANT),
        name="legendre_sums",
    )(wave_order, moved, table)


def solution(mesh):
    placed = (P(None, None, "lat", "lon"), P(("lat", "lon"), None, None), P())
    return jax.shard_map(
        on_device,
        mesh=mesh,
        in_specs=placed,
        out_specs=P(("lat", "lon"), None, None, None),
        check_vma=False,
    )
```

```python
import functools
import itertools
import math

import jax
import jax.numpy as jnp
import numpy as np
from jax import lax
from jax.experimental import pallas as pl
from jax.experimental.pallas import tpu as pltpu
from jax.sharding import PartitionSpec as P

NLON = 8192
MW = 2048
BLOCKS = 16
SPAN = NLON // BLOCKS
HALF = MW // BLOCKS
CIRCLES = 64
ROWS = 16
MESH = pl.DeviceIdType.MESH


@functools.cache
def tables():
    n = np.arange(SPAN)
    wave = np.arange(HALF)
    phase = 2.0 * np.pi / (2 * SPAN) * (n[None, :] * (2 * wave[:, None] + 1) % (2 * SPAN))
    basis = np.concatenate([np.cos(phase), np.sin(phase)]) / math.sqrt(NLON)
    high = basis.astype(jnp.bfloat16)
    low = (basis - high.astype(np.float64)).astype(jnp.bfloat16)
    first = np.arange(BLOCKS // 2 + 1) - BLOCKS // 2
    angle = 2.0 * np.pi / NLON * (n[None, :] * first[:, None])
    twiddle = np.zeros((24, SPAN), np.float32)
    twiddle[0:9] = np.cos(angle)
    twiddle[9:18] = -np.sin(angle)
    return np.concatenate([high, low]), twiddle


def real_dft(xs):
    n = len(xs)
    if n == 2:
        return [(xs[0] + xs[1], None), (xs[0] - xs[1], None)]
    evens, odds = real_dft(xs[0::2]), real_dft(xs[1::2])
    out = [None] * (n // 2 + 1)
    for k in range(n // 4 + 1):
        (er, ei), (orr, oi) = evens[k], odds[k]
        if k == 0:
            out[0], out[n // 2] = (er + orr, None), (er - orr, None)
        elif k == n // 4:
            out[k] = (er, -orr)
        else:
            c, s = math.cos(2 * math.pi * k / n), math.sin(2 * math.pi * k / n)
            tr, ti = (c * orr, -s * orr) if oi is None else (c * orr + s * oi, c * oi - s * orr)
            out[k] = (er + tr, ti if ei is None else ei + ti)
            out[n // 2 - k] = (er - tr, ti if ei is None else ti - ei)
    return out


def split(x):
    high = x.astype(jnp.bfloat16)
    return high, (x - high.astype(jnp.float32)).astype(jnp.bfloat16)


NT = (((1,), (1,)), ((), ()))
CHUNKS = 4
CROWS = CIRCLES // CHUNKS
HALVES = 2
GRANT = 49_737_728
ZROWS = 10 * 64


def fourier_kernel(
    lat_n, lon_n, order_hbm, v_hbm, basis_hbm, twiddle_hbm, table_hbm, out_ref, table_ref,
    order, v_in, basis, twiddle, sent, got, z_high, z_low, fourier, picked, packed,
    load_sem, send_sem, recv_sem, own_sem, out_send, out_recv, out_own,
):
    lat, lon = lax.axis_index("lat"), lax.axis_index("lon")
    x, core, y, z = lat // 2, lax.rem(lat, 2), lon // 4, lax.rem(lon, 4)
    ring = (2, 1, 3, 0)
    xs, ys, zs = ([lax.rem(at + d, 4) for d in range(4)] for at in (x, y, z))
    cores = [core, 1 - core]
    hops = lambda *shift: -sum(min(d, 4 - d) for d in shift)
    plane = sorted([(dy, dz) for dy in ring for dz in ring if dy or dz], key=lambda s: hops(*s))
    peers = [ys[dy] * 4 + zs[dz] for dy, dz in plane]

    barrier = pltpu.get_barrier_semaphore()
    for peer in peers:
        pl.semaphore_signal(barrier, inc=1, device_id=(lat, peer), device_id_type=MESH)
    for dx, dc in itertools.product(ring, (1, 0)):
        if dx or dc:
            pl.semaphore_signal(barrier, inc=1, device_id=(xs[dx] * 2 + cores[dc], lon), device_id_type=MESH)

    v_copy = pltpu.make_async_copy(v_hbm, v_in, load_sem.at[0])
    v_copy.start()
    basis_copy = pltpu.make_async_copy(basis_hbm, basis, load_sem.at[1])
    basis_copy.start()
    order_copy = pltpu.make_async_copy(order_hbm, order, load_sem.at[3])
    order_copy.start()
    twiddle_copy = pltpu.make_async_copy(twiddle_hbm, twiddle, load_sem.at[4])
    twiddle_copy.start()

    v_copy.wait()
    table_copy = pltpu.make_async_copy(table_hbm, table_ref, load_sem.at[2])
    table_copy.start()

    @pl.loop(0, lon_n)
    def _(level):
        for c in range(CHUNKS):
            h, j = divmod(c * CROWS, 32)
            sent[level, c] = v_in[level, h, j : j + CROWS, :].astype(jnp.bfloat16)

    own = pltpu.make_async_copy(sent.at[lon], got.at[lon], own_sem)
    own.start()
    pl.semaphore_wait(barrier, lon_n - 1 + lat_n - 1)

    for c in range(CHUNKS):
        for peer in peers:
            pltpu.make_async_remote_copy(
                src_ref=sent.at[peer, c],
                dst_ref=got.at[lon, c],
                send_sem=send_sem,
                recv_sem=recv_sem.at[c],
                device_id=(lat, peer),
                device_id_type=MESH,
            ).start()

    basis_copy.wait()
    order_copy.wait()
    twiddle_copy.wait()
    own.wait()
    me = lat * lon_n + lon
    lane = lax.broadcasted_iota(jnp.int32, (1, 128), 1)
    real = lax.rem(lane, 64) < 32
    sign = jnp.where(real, 1.0, -1.0).astype(jnp.float32)
    for half in range(HALVES):
        empty = pl.ds(half * ZROWS + 17 * 32, ZROWS - 17 * 32)
        z_high[empty, :] = jnp.zeros((ZROWS - 17 * 32, SPAN), jnp.bfloat16)
        z_low[empty, :] = jnp.zeros((ZROWS - 17 * 32, SPAN), jnp.bfloat16)

    def first_stage(c):
        pltpu.make_async_copy(got.at[pl.ds(1, lon_n - 1), c], got.at[pl.ds(1, lon_n - 1), c], recv_sem.at[c]).wait()
        half, part_of_half = divmod(c, CHUNKS // HALVES)

        @pl.loop(0, SPAN // 128)
        def _(part):
            lanes = pl.ds(pl.multiple_of(part * 128, 128), 128)
            blocks = [got[b, c, :, lanes].astype(jnp.float32) for b in range(BLOCKS)]
            for k, (yr, yi) in enumerate(real_dft(blocks)):
                row = half * ZROWS + k * 64 + part_of_half * CROWS
                if k == BLOCKS // 2:
                    zs = [yr]
                else:
                    tc, ts = twiddle[k : k + 1, lanes], twiddle[k + 9 : k + 10, lanes]
                    if yi is None:
                        zs = [yr * tc, yr * ts]
                    else:
                        zs = [yr * tc - yi * ts, yr * ts + yi * tc]
                for i, z_part in enumerate(zs):
                    high, low = split(z_part)
                    z_high[pl.ds(row + i * 32, CROWS), lanes] = high
                    z_low[pl.ds(row + i * 32, CROWS), lanes] = low

    def second_stage(half):
        for k0, count in ((0, 4), (4, 4), (8, 2)):
            rows = pl.ds(half * ZROWS + k0 * 64, count * 64)
            by_high = lax.dot_general(basis[...], z_high[rows, :], NT, preferred_element_type=jnp.float32)
            by_low = lax.dot_general(basis[: 2 * HALF, :], z_low[rows, :], NT, preferred_element_type=jnp.float32)
            both = by_high[: 2 * HALF] + by_high[2 * HALF :] + by_low
            for pair in range(count // 2):
                at = slice(pair * 128, pair * 128 + 128)
                cos_part, sin_part = both[:HALF, at], both[HALF:, at]
                swapped = jnp.where(real, pltpu.roll(sin_part, 96, 1), pltpu.roll(sin_part, 32, 1))
                plus, minus = cos_part + sign * swapped, sign * cos_part - swapped
                k = k0 + pair * 2
                for value, first, second in ((plus, k, k + 1), (minus, BLOCKS - k, BLOCKS - k - 1)):
                    turned = pltpu.roll(value, 64, 1)
                    for wave, row in ((first, jnp.where(lane < 64, value, turned)), (second, jnp.where(lane < 64, turned, value))):
                        if (wave <= BLOCKS // 2) if value is plus else (BLOCKS // 2 < wave < BLOCKS):
                            fourier[pl.ds(wave, HALF, stride=BLOCKS), :] = row

    def gather(half, group):
        dx, dy = groups[group]

        @pl.loop(0, 2)
        def _(t):
            for u in range(4):
                to_z, to_core = lax.rem(z + t * 2 + u // 2, 4), cores[u % 2]
                base = ((xs[dx] * 2 + to_core) * lon_n + ys[dy] * 4 + to_z) * ROWS
                here = pl.multiple_of((group * 8 + t * 4 + u) * ROWS, ROWS)
                for r in range(ROWS):
                    picked[pl.ds(here + r, 1), :] = fourier[pl.ds(order[base + r], 1), :]
            for u in range(4):
                here = pl.multiple_of((group * 8 + t * 4 + u) * ROWS, ROWS)
                pair = jnp.where(lane < 64, picked[pl.ds(here, 8), :], picked[pl.ds(here + 8, 8), :])
                packed[half, group * 8 + t * 4 + u] = pair.astype(jnp.bfloat16)

    def send(half, group):
        dx, dy = groups[group]
        for dz, dc in itertools.product(ring, (1, 0)):
            message = packed.at[half, group * 8 + dz * 2 + dc]
            if dx or dy or dz or dc:
                pltpu.make_async_remote_copy(
                    src_ref=message,
                    dst_ref=out_ref.at[half, me],
                    send_sem=out_send,
                    recv_sem=out_recv,
                    device_id=(xs[dx] * 2 + cores[dc], ys[dy] * 4 + zs[dz]),
                    device_id_type=MESH,
                ).start()
            else:
                pltpu.make_async_copy(message, out_ref.at[half, me], out_own.at[half]).start()

    groups = list(itertools.product(ring, ring))
    for c in range(CHUNKS // 2):
        first_stage(c)
    second_stage(0)
    for g in range(16):
        gather(0, g)
    for c in range(CHUNKS // 2, CHUNKS - 1):
        first_stage(c)
    for g in range(16):
        send(0, g)
    first_stage(CHUNKS - 1)
    second_stage(1)
    for g in range(16):
        gather(1, g)
        send(1, g)

    blocks = sent.at[pl.ds(1, lon_n - 1)]
    pltpu.make_async_copy(blocks, blocks, send_sem).wait()
    for half in range(HALVES):
        pltpu.make_async_copy(packed.at[half, 0], out_ref.at[half, me], out_own.at[half]).wait()
    rest = packed.at[:, pl.ds(0, lat_n * lon_n - 1)]
    pltpu.make_async_copy(rest, rest, out_send).wait()
    pltpu.make_async_copy(rest, rest, out_recv).wait()
    table_copy.wait()


KB = 256


def prepare(moved, data, r, half):
    lane = lax.broadcasted_iota(jnp.int32, (16, 128), 1) // 32
    for k in range(2):
        xs = [moved[pl.ds(half * 1024 + (k * 4 + i) * 128 + r, 16, stride=8), :] for i in range(4)]
        for g in range(4):
            rolled = [x if i == g else pltpu.roll(x, (i - g) % 4 * 32, 1) for i, x in enumerate(xs)]
            low = jnp.where(lane < 1, rolled[0], rolled[1])
            high = jnp.where(lane < 3, rolled[2], rolled[3])
            rows = pl.ds(pl.multiple_of((g % 2 * 2 + half) * 16, 16), 16)
            data[g // 2 * 8 + r, rows, pl.ds(k * 128, 128)] = jnp.where(lane < 2, low, high).astype(jnp.bfloat16)


def legendre_kernel(order_hbm, moved_ref, table_in, out, order, moved, data, result, zeros, order_sem, out_sem):
    slots, degrees, lats = table_in.shape
    parts = degrees // KB
    first = (lax.axis_index("lat") * lax.axis_size("lon") + lax.axis_index("lon")) * slots

    def blocks(s):
        return (degrees - order[first + s] + KB - 1) // KB

    order_copy = pltpu.make_async_copy(order_hbm, order, order_sem)
    order_copy.start()
    zeros[...] = jnp.zeros_like(zeros)

    for half in range(HALVES):

        @pl.loop(0, 128 // 16)
        def _(group):
            for i in range(16):
                source = group * 16 + i
                row = pl.multiple_of(half * 1024 + source * 8, 8)
                moved[pl.ds(row, 8), :] = moved_ref[half, source].astype(jnp.float32)

        prepare(moved, data, 0, half)

    order_copy.wait()

    @pl.loop(0, slots)
    def _(t):
        half, pair = lax.rem(t, 2), t // 2
        s = half * 8 + pair
        count = blocks(s)
        limit = degrees - order[first + s]
        for p in range(1, parts + 1):

            @pl.when(count == p)
            def _():
                for q in range(p):
                    at = pl.ds(q * KB, KB)
                    sums = lax.dot_general(data[s], table_in[s, at, :], NT, preferred_element_type=jnp.float32)
                    degree = lax.broadcasted_iota(jnp.int32, (1, KB), 1)
                    parity = (1 - 2 * (degree % 2)).astype(jnp.float32)
                    for c in range(2):
                        both = sums[c * 32 : c * 32 + 16] + parity * sums[c * 32 + 16 : c * 32 + 32]
                        if q == p - 1:
                            both = jnp.where(degree + q * KB < limit, both, 0.0)
                        result[s, c, :, at] = both
                prepare(moved, data, lax.rem(pair + 1, 8), half)
                used = pl.ds(0, p * KB)
                pltpu.make_async_copy(result.at[s, :, :, used], out.at[s, :, :, used], out_sem).start()
                if p < parts:
                    rest = pl.ds(p * KB, degrees - p * KB)
                    pltpu.make_async_copy(zeros.at[:, :, rest], out.at[s, :, :, rest], out_sem).start()

    pltpu.make_async_copy(result, out, out_sem).wait()


def on_device(vorticity, legendre, wave_order):
    lat_n, lon_n = lax.axis_size("lat"), lax.axis_size("lon")
    n = lat_n * lon_n
    basis, twiddle = tables()
    bf16, f32 = jnp.bfloat16, jnp.float32
    hbm = pl.BlockSpec(memory_space=pl.ANY)
    vmem = pl.BlockSpec(memory_space=pltpu.VMEM)
    dma = pltpu.SemaphoreType.DMA
    moved, table = pl.pallas_call(
        functools.partial(fourier_kernel, lat_n, lon_n),
        out_shape=(pltpu.VMEM((HALVES, n, ROWS // 2, 128), bf16), pltpu.VMEM(legendre.shape, bf16)),
        in_specs=[hbm, hbm, hbm, hbm, hbm],
        out_specs=(vmem, vmem),
        scratch_shapes=[
            pltpu.SMEM(wave_order.shape, jnp.int32),
            pltpu.VMEM(vorticity.shape, f32),
            pltpu.VMEM(basis.shape, bf16),
            pltpu.VMEM(twiddle.shape, f32),
            pltpu.VMEM((lon_n, CHUNKS, CROWS, SPAN), bf16),
            pltpu.VMEM((lon_n, CHUNKS, CROWS, SPAN), bf16),
            pltpu.VMEM((HALVES * ZROWS, SPAN), bf16),
            pltpu.VMEM((HALVES * ZROWS, SPAN), bf16),
            pltpu.VMEM((MW, 128), f32),
            pltpu.VMEM((MW, 128), f32),
            pltpu.VMEM((HALVES, n, ROWS // 2, 128), bf16),
            dma((5,)),
            dma,
            dma((CHUNKS,)),
            dma,
            dma,
            dma,
            dma((HALVES,)),
        ],
        compiler_params=pltpu.CompilerParams(collective_id=0, has_side_effects=True, vmem_limit_bytes=GRANT),
        name="fourier",
    )(wave_order, vorticity, jnp.asarray(basis), jnp.asarray(twiddle), legendre)

    slots, degrees, lats = legendre.shape
    moved = pltpu.with_memory_space_constraint(moved, pltpu.VMEM)
    table = pltpu.with_memory_space_constraint(table, pltpu.VMEM)
    return pl.pallas_call(
        legendre_kernel,
        out_shape=jax.ShapeDtypeStruct((slots, 2, 16, degrees), f32),
        in_specs=[hbm, vmem, vmem],
        out_specs=hbm,
        scratch_shapes=[
            pltpu.SMEM(wave_order.shape, jnp.int32),
            pltpu.VMEM((MW, 128), f32),
            pltpu.VMEM((slots, 64, lats), bf16),
            pltpu.VMEM((slots, 2, 16, degrees), f32),
            pltpu.VMEM((2, 16, degrees), f32),
            dma,
            dma,
        ],
        compiler_params=pltpu.CompilerParams(vmem_limit_bytes=GRANT),
        name="legendre_sums",
    )(wave_order, moved, table)


def solution(mesh):
    placed = (P(None, None, "lat", "lon"), P(("lat", "lon"), None, None), P())
    return jax.shard_map(
        on_device,
        mesh=mesh,
        in_specs=placed,
        out_specs=P(("lat", "lon"), None, None, None),
        check_vma=False,
    )
```

```python
import functools
import itertools
import math

import jax
import jax.numpy as jnp
import numpy as np
from jax import lax
from jax.experimental import pallas as pl
from jax.experimental.pallas import tpu as pltpu
from jax.sharding import PartitionSpec as P

NLON = 8192
MW = 2048
BLOCKS = 16
SPAN = NLON // BLOCKS
HALF = MW // BLOCKS
CIRCLES = 64
ROWS = 16
MESH = pl.DeviceIdType.MESH


@functools.cache
def tables():
    n = np.arange(SPAN)
    wave = np.arange(HALF)
    phase = 2.0 * np.pi / (2 * SPAN) * (n[None, :] * (2 * wave[:, None] + 1) % (2 * SPAN))
    basis = np.concatenate([np.cos(phase), np.sin(phase)]) / math.sqrt(NLON)
    high = basis.astype(jnp.bfloat16)
    low = (basis - high.astype(np.float64)).astype(jnp.bfloat16)
    first = np.arange(BLOCKS // 2 + 1) - BLOCKS // 2
    angle = 2.0 * np.pi / NLON * (n[None, :] * first[:, None])
    twiddle = np.zeros((24, SPAN), np.float32)
    twiddle[0:9] = np.cos(angle)
    twiddle[9:18] = -np.sin(angle)
    return np.concatenate([high, low]), twiddle


def real_dft(xs):
    n = len(xs)
    if n == 2:
        return [(xs[0] + xs[1], None), (xs[0] - xs[1], None)]
    evens, odds = real_dft(xs[0::2]), real_dft(xs[1::2])
    out = [None] * (n // 2 + 1)
    for k in range(n // 4 + 1):
        (er, ei), (orr, oi) = evens[k], odds[k]
        if k == 0:
            out[0], out[n // 2] = (er + orr, None), (er - orr, None)
        elif k == n // 4:
            out[k] = (er, -orr)
        else:
            c, s = math.cos(2 * math.pi * k / n), math.sin(2 * math.pi * k / n)
            tr, ti = (c * orr, -s * orr) if oi is None else (c * orr + s * oi, c * oi - s * orr)
            out[k] = (er + tr, ti if ei is None else ei + ti)
            out[n // 2 - k] = (er - tr, ti if ei is None else ti - ei)
    return out


def split(x):
    high = x.astype(jnp.bfloat16)
    return high, (x - high.astype(jnp.float32)).astype(jnp.bfloat16)


NT = (((1,), (1,)), ((), ()))
CHUNKS = 4
CROWS = CIRCLES // CHUNKS
HALVES = 2
GRANT = 49_737_728
ZROWS = 10 * 64


def fourier_kernel(
    lat_n, lon_n, order_hbm, v_hbm, basis_hbm, twiddle_hbm, table_hbm, out_ref, table_ref,
    order, v_in, basis, twiddle, sent, got, z_high, z_low, fourier, picked, packed,
    load_sem, send_sem, recv_sem, own_sem, out_send, out_recv, out_own,
):
    lat, lon = lax.axis_index("lat"), lax.axis_index("lon")
    x, core, y, z = lat // 2, lax.rem(lat, 2), lon // 4, lax.rem(lon, 4)
    ring = (2, 1, 3, 0)
    xs, ys, zs = ([lax.rem(at + d, 4) for d in range(4)] for at in (x, y, z))
    cores = [core, 1 - core]
    hops = lambda *shift: -sum(min(d, 4 - d) for d in shift)
    plane = sorted([(dy, dz) for dy in ring for dz in ring if dy or dz], key=lambda s: hops(*s))
    peers = [ys[dy] * 4 + zs[dz] for dy, dz in plane]

    barrier = pltpu.get_barrier_semaphore()
    for peer in peers:
        pl.semaphore_signal(barrier, inc=1, device_id=(lat, peer), device_id_type=MESH)
    for dx, dc in itertools.product(ring, (1, 0)):
        if dx or dc:
            pl.semaphore_signal(barrier, inc=1, device_id=(xs[dx] * 2 + cores[dc], lon), device_id_type=MESH)

    v_copy = pltpu.make_async_copy(v_hbm, v_in, load_sem.at[0])
    v_copy.start()
    basis_copy = pltpu.make_async_copy(basis_hbm, basis, load_sem.at[1])
    basis_copy.start()
    order_copy = pltpu.make_async_copy(order_hbm, order, load_sem.at[3])
    order_copy.start()
    twiddle_copy = pltpu.make_async_copy(twiddle_hbm, twiddle, load_sem.at[4])
    twiddle_copy.start()

    v_copy.wait()
    table_copy = pltpu.make_async_copy(table_hbm, table_ref, load_sem.at[2])
    table_copy.start()

    @pl.loop(0, lon_n)
    def _(level):
        for c in range(CHUNKS):
            h, j = divmod(c * CROWS, 32)
            sent[level, c] = v_in[level, h, j : j + CROWS, :].astype(jnp.bfloat16)

    own = pltpu.make_async_copy(sent.at[lon], got.at[lon], own_sem)
    own.start()
    pl.semaphore_wait(barrier, lon_n - 1 + lat_n - 1)

    for c in range(CHUNKS):
        for peer in peers:
            pltpu.make_async_remote_copy(
                src_ref=sent.at[peer, c],
                dst_ref=got.at[lon, c],
                send_sem=send_sem,
                recv_sem=recv_sem.at[c],
                device_id=(lat, peer),
                device_id_type=MESH,
            ).start()

    basis_copy.wait()
    order_copy.wait()
    twiddle_copy.wait()
    own.wait()
    me = lat * lon_n + lon
    lane = lax.broadcasted_iota(jnp.int32, (1, 128), 1)
    real = lax.rem(lane, 64) < 32
    sign = jnp.where(real, 1.0, -1.0).astype(jnp.float32)
    for half in range(HALVES):
        empty = pl.ds(half * ZROWS + 17 * 32, ZROWS - 17 * 32)
        z_high[empty, :] = jnp.zeros((ZROWS - 17 * 32, SPAN), jnp.bfloat16)
        z_low[empty, :] = jnp.zeros((ZROWS - 17 * 32, SPAN), jnp.bfloat16)

    def first_stage(c):
        pltpu.make_async_copy(got.at[pl.ds(1, lon_n - 1), c], got.at[pl.ds(1, lon_n - 1), c], recv_sem.at[c]).wait()
        half, part_of_half = divmod(c, CHUNKS // HALVES)

        @pl.loop(0, SPAN // 128)
        def _(part):
            lanes = pl.ds(pl.multiple_of(part * 128, 128), 128)
            blocks = [got[b, c, :, lanes].astype(jnp.float32) for b in range(BLOCKS)]
            for k, (yr, yi) in enumerate(real_dft(blocks)):
                row = half * ZROWS + k * 64 + part_of_half * CROWS
                if k == BLOCKS // 2:
                    zs = [yr]
                else:
                    tc, ts = twiddle[k : k + 1, lanes], twiddle[k + 9 : k + 10, lanes]
                    if yi is None:
                        zs = [yr * tc, yr * ts]
                    else:
                        zs = [yr * tc - yi * ts, yr * ts + yi * tc]
                for i, z_part in enumerate(zs):
                    high, low = split(z_part)
                    z_high[pl.ds(row + i * 32, CROWS), lanes] = high
                    z_low[pl.ds(row + i * 32, CROWS), lanes] = low

    def second_stage(half):
        for k0, count in ((0, 4), (4, 4), (8, 2)):
            rows = pl.ds(half * ZROWS + k0 * 64, count * 64)
            by_high = lax.dot_general(basis[...], z_high[rows, :], NT, preferred_element_type=jnp.float32)
            by_low = lax.dot_general(basis[: 2 * HALF, :], z_low[rows, :], NT, preferred_element_type=jnp.float32)
            both = by_high[: 2 * HALF] + by_high[2 * HALF :] + by_low
            for pair in range(count // 2):
                at = slice(pair * 128, pair * 128 + 128)
                cos_part, sin_part = both[:HALF, at], both[HALF:, at]
                swapped = jnp.where(real, pltpu.roll(sin_part, 96, 1), pltpu.roll(sin_part, 32, 1))
                plus, minus = cos_part + sign * swapped, sign * cos_part - swapped
                k = k0 + pair * 2
                for value, first, second in ((plus, k, k + 1), (minus, BLOCKS - k, BLOCKS - k - 1)):
                    turned = pltpu.roll(value, 64, 1)
                    for wave, row in ((first, jnp.where(lane < 64, value, turned)), (second, jnp.where(lane < 64, turned, value))):
                        if (wave <= BLOCKS // 2) if value is plus else (BLOCKS // 2 < wave < BLOCKS):
                            fourier[pl.ds(wave, HALF, stride=BLOCKS), :] = row

    def gather(half, group):
        dx, dy = groups[group]

        @pl.loop(0, 2)
        def _(t):
            for u in range(4):
                to_z, to_core = lax.rem(z + t * 2 + u // 2, 4), cores[u % 2]
                base = ((xs[dx] * 2 + to_core) * lon_n + ys[dy] * 4 + to_z) * ROWS
                here = pl.multiple_of((group * 8 + t * 4 + u) * ROWS, ROWS)
                for r in range(ROWS):
                    picked[pl.ds(here + r, 1), :] = fourier[pl.ds(order[base + r], 1), :]
            for u in range(4):
                here = pl.multiple_of((group * 8 + t * 4 + u) * ROWS, ROWS)
                pair = jnp.where(lane < 64, picked[pl.ds(here, 8), :], picked[pl.ds(here + 8, 8), :])
                packed[half, group * 8 + t * 4 + u] = pair.astype(jnp.bfloat16)

    def send(half, group):
        dx, dy = groups[group]
        for dz, dc in itertools.product(ring, (1, 0)):
            message = packed.at[half, group * 8 + dz * 2 + dc]
            if dx or dy or dz or dc:
                pltpu.make_async_remote_copy(
                    src_ref=message,
                    dst_ref=out_ref.at[half, me],
                    send_sem=out_send,
                    recv_sem=out_recv,
                    device_id=(xs[dx] * 2 + cores[dc], ys[dy] * 4 + zs[dz]),
                    device_id_type=MESH,
                ).start()
            else:
                pltpu.make_async_copy(message, out_ref.at[half, me], out_own.at[half]).start()

    groups = sorted(itertools.product(ring, ring), key=lambda s: hops(*s))
    for c in range(CHUNKS // 2):
        first_stage(c)
    second_stage(0)
    for g in range(16):
        gather(0, g)
    for c in range(CHUNKS // 2, CHUNKS - 1):
        first_stage(c)
    for g in range(16):
        send(0, g)
    first_stage(CHUNKS - 1)
    second_stage(1)
    for g in range(16):
        gather(1, g)
        send(1, g)

    blocks = sent.at[pl.ds(1, lon_n - 1)]
    pltpu.make_async_copy(blocks, blocks, send_sem).wait()
    for half in range(HALVES):
        pltpu.make_async_copy(packed.at[half, 0], out_ref.at[half, me], out_own.at[half]).wait()
    rest = packed.at[:, pl.ds(0, lat_n * lon_n - 1)]
    pltpu.make_async_copy(rest, rest, out_send).wait()
    pltpu.make_async_copy(rest, rest, out_recv).wait()
    table_copy.wait()


KB = 256


def prepare(moved, data, r, half):
    lane = lax.broadcasted_iota(jnp.int32, (16, 128), 1) // 32
    for k in range(2):
        xs = [moved[pl.ds(half * 1024 + (k * 4 + i) * 128 + r, 16, stride=8), :] for i in range(4)]
        for g in range(4):
            rolled = [x if i == g else pltpu.roll(x, (i - g) % 4 * 32, 1) for i, x in enumerate(xs)]
            low = jnp.where(lane < 1, rolled[0], rolled[1])
            high = jnp.where(lane < 3, rolled[2], rolled[3])
            rows = pl.ds(pl.multiple_of((g % 2 * 2 + half) * 16, 16), 16)
            data[g // 2 * 8 + r, rows, pl.ds(k * 128, 128)] = jnp.where(lane < 2, low, high).astype(jnp.bfloat16)


def legendre_kernel(order_hbm, moved_ref, table_in, out, order, moved, data, result, zeros, order_sem, out_sem):
    slots, degrees, lats = table_in.shape
    parts = degrees // KB
    first = (lax.axis_index("lat") * lax.axis_size("lon") + lax.axis_index("lon")) * slots

    def blocks(s):
        return (degrees - order[first + s] + KB - 1) // KB

    order_copy = pltpu.make_async_copy(order_hbm, order, order_sem)
    order_copy.start()
    zeros[...] = jnp.zeros_like(zeros)

    for half in range(HALVES):

        @pl.loop(0, 128 // 16)
        def _(group):
            for i in range(16):
                source = group * 16 + i
                row = pl.multiple_of(half * 1024 + source * 8, 8)
                moved[pl.ds(row, 8), :] = moved_ref[half, source].astype(jnp.float32)

        prepare(moved, data, 0, half)

    order_copy.wait()

    @pl.loop(0, slots)
    def _(t):
        half, pair = lax.rem(t, 2), t // 2
        s = half * 8 + pair
        count = blocks(s)
        limit = degrees - order[first + s]
        for p in range(1, parts + 1):

            @pl.when(count == p)
            def _():
                for q in range(p):
                    at = pl.ds(q * KB, KB)
                    sums = lax.dot_general(data[s], table_in[s, at, :], NT, preferred_element_type=jnp.float32)
                    degree = lax.broadcasted_iota(jnp.int32, (1, KB), 1)
                    parity = (1 - 2 * (degree % 2)).astype(jnp.float32)
                    for c in range(2):
                        both = sums[c * 32 : c * 32 + 16] + parity * sums[c * 32 + 16 : c * 32 + 32]
                        if q == p - 1:
                            both = jnp.where(degree + q * KB < limit, both, 0.0)
                        result[s, c, :, at] = both
                prepare(moved, data, lax.rem(pair + 1, 8), half)
                used = pl.ds(0, p * KB)
                pltpu.make_async_copy(result.at[s, :, :, used], out.at[s, :, :, used], out_sem).start()
                if p < parts:
                    rest = pl.ds(p * KB, degrees - p * KB)
                    pltpu.make_async_copy(zeros.at[:, :, rest], out.at[s, :, :, rest], out_sem).start()

    pltpu.make_async_copy(result, out, out_sem).wait()


def on_device(vorticity, legendre, wave_order):
    lat_n, lon_n = lax.axis_size("lat"), lax.axis_size("lon")
    n = lat_n * lon_n
    basis, twiddle = tables()
    bf16, f32 = jnp.bfloat16, jnp.float32
    hbm = pl.BlockSpec(memory_space=pl.ANY)
    vmem = pl.BlockSpec(memory_space=pltpu.VMEM)
    dma = pltpu.SemaphoreType.DMA
    moved, table = pl.pallas_call(
        functools.partial(fourier_kernel, lat_n, lon_n),
        out_shape=(pltpu.VMEM((HALVES, n, ROWS // 2, 128), bf16), pltpu.VMEM(legendre.shape, bf16)),
        in_specs=[hbm, hbm, hbm, hbm, hbm],
        out_specs=(vmem, vmem),
        scratch_shapes=[
            pltpu.SMEM(wave_order.shape, jnp.int32),
            pltpu.VMEM(vorticity.shape, f32),
            pltpu.VMEM(basis.shape, bf16),
            pltpu.VMEM(twiddle.shape, f32),
            pltpu.VMEM((lon_n, CHUNKS, CROWS, SPAN), bf16),
            pltpu.VMEM((lon_n, CHUNKS, CROWS, SPAN), bf16),
            pltpu.VMEM((HALVES * ZROWS, SPAN), bf16),
            pltpu.VMEM((HALVES * ZROWS, SPAN), bf16),
            pltpu.VMEM((MW, 128), f32),
            pltpu.VMEM((MW, 128), f32),
            pltpu.VMEM((HALVES, n, ROWS // 2, 128), bf16),
            dma((5,)),
            dma,
            dma((CHUNKS,)),
            dma,
            dma,
            dma,
            dma((HALVES,)),
        ],
        compiler_params=pltpu.CompilerParams(collective_id=0, has_side_effects=True, vmem_limit_bytes=GRANT),
        name="fourier",
    )(wave_order, vorticity, jnp.asarray(basis), jnp.asarray(twiddle), legendre)

    slots, degrees, lats = legendre.shape
    moved = pltpu.with_memory_space_constraint(moved, pltpu.VMEM)
    table = pltpu.with_memory_space_constraint(table, pltpu.VMEM)
    return pl.pallas_call(
        legendre_kernel,
        out_shape=jax.ShapeDtypeStruct((slots, 2, 16, degrees), f32),
        in_specs=[hbm, vmem, vmem],
        out_specs=hbm,
        scratch_shapes=[
            pltpu.SMEM(wave_order.shape, jnp.int32),
            pltpu.VMEM((MW, 128), f32),
            pltpu.VMEM((slots, 64, lats), bf16),
            pltpu.VMEM((slots, 2, 16, degrees), f32),
            pltpu.VMEM((2, 16, degrees), f32),
            dma,
            dma,
        ],
        compiler_params=pltpu.CompilerParams(vmem_limit_bytes=GRANT),
        name="legendre_sums",
    )(wave_order, moved, table)


def solution(mesh):
    placed = (P(None, None, "lat", "lon"), P(("lat", "lon"), None, None), P())
    return jax.shard_map(
        on_device,
        mesh=mesh,
        in_specs=placed,
        out_specs=P(("lat", "lon"), None, None, None),
        check_vma=False,
    )
```
